32 devices in a mesh: grp: 4 (over x, core), rows: 8 (over z, y).
Axes of the slice: x: 2, y: 2, z: 4, core: 2. Of those that a mesh axis runs over, the one named last changes fastest.
Arguments:
- table_rows: bfloat16 [8, 2048, 768], P('rows', 'grp'), may hold values from -6 to 6
- cotangent: bfloat16 [8, 2048, 768], P('rows', 'grp'), may hold values from -6 to 6
- w_query: bfloat16 [768, 768], replicated, may hold values from -0.21875 to 0.21875
- w_key: bfloat16 [768, 768], replicated, may hold values from -0.21875 to 0.21875
- w_value: bfloat16 [768, 768], replicated, may hold values from -0.21875 to 0.21875
- w_out: bfloat16 [768, 768], replicated, may hold values from -1.75 to 1.75
- w_up: bfloat16 [768, 3072], replicated, may hold values from -0.21875 to 0.21875
- w_down: bfloat16 [3072, 768], replicated, may hold values from -0.109375 to 0.109375
- b_up: float32 [3072], replicated, may hold values from -3 to 3
- b_down: float32 [768], replicated, may hold values from -2 to 2
- g_one: float32 [768], replicated, may hold values from 0.5 to 1.5
- b_one: float32 [768], replicated, may hold values from -2 to 2
- g_two: float32 [768], replicated, may hold values from 0.5 to 1.5
- b_two: float32 [768], replicated, may hold values from -2 to 2
- ctx_count: int32 [8], P('rows'), may hold values from 1024 to 1536
- qry_count: int32 [8], P('rows'), may hold values from 256 to 512
- key_keep: int32 [8, 2048], P('rows'), may hold values from 0 to 1
Outputs:
- result: bfloat16 [8, 2048, 768], P('rows', 'grp')
- d_rows: bfloat16 [8, 2048, 768], P('rows', 'grp')
- d_w_query: float32 [768, 768], replicated
- d_w_key: float32 [768, 768], replicated
- d_w_value: float32 [768, 768], replicated
- d_w_out: float32 [768, 768], replicated
- d_w_up: float32 [768, 3072], replicated
- d_w_down: float32 [3072, 768], replicated
- d_b_up: float32 [3072], replicated
- d_b_down: float32 [768], replicated
- d_g_one: float32 [768], replicated
- d_b_one: float32 [768], replicated
- d_g_two: float32 [768], replicated
- d_b_two: float32 [768], replicated
The draws below stay inside these ranges and needn't reach their ends.
All inputs are finite; a program needn't handle non-finite values.
Results may differ from the reference program's by a relative error of at most 0.013.
Values may be sent and summed in bfloat16 or wider, within the bound.
No kernel may reach another device: no remote copies, remote signals or barrier semaphores. Data moves between devices by JAX's collectives and lax.ppermute only.
A program may use at most 320 MiB of HBM per device.

```python
import jax
import jax.numpy as jnp
from jax import lax

D = 768
H = 12
DH = 64
FF = 3072
SLOTS = 2048
TABLES = 8


def draw_key_keep(key, part):
    levels = jax.random.randint(key, (TABLES, SLOTS), 0, 8)
    kept = (levels != 0).astype(jnp.int32)
    return kept.at[:, 0].set(1)


def touch_ends(array, rng, smallest, largest):
    extent = array.shape
    place = [jax.random.randint(jax.random.fold_in(rng, axis), (), 0, extent[axis]) for axis in range(len(extent))]
    array = array.at[tuple(place)].set(smallest)
    longest = extent.index(max(extent))
    place[longest] = (place[longest] + 1) % extent[longest]
    return array.at[tuple(place)].set(largest)


def level_of(own_key, shape, cuts, least, high):
    def one(dim, blocks):
        heights = jax.random.uniform(jax.random.fold_in(jax.random.fold_in(own_key, 6), dim), (blocks,), jnp.float32, least / len(cuts), high / len(cuts))
        return jnp.repeat(jnp.exp(heights), shape[dim] // blocks).reshape((-1,) + (1,) * (len(shape) - dim - 1))

    level = one(*cuts[0])
    for cut in cuts[1:]:
        level = level * one(*cut)
    return level


def scatter_about(stream_key, extent, scale, most, split=(), held_as=jnp.bfloat16):
    drawn = scale * jax.random.normal(stream_key, extent, jnp.float32)
    if split:
        drawn = drawn * level_of(stream_key, extent, split, -0.22, 0.18)
    return jnp.clip(drawn, -most, most).astype(held_as)


def setup_inputs(seed: int = 0) -> dict:
    keys = jax.random.split(jax.random.key(seed), 18)
    return {
        "table_rows": scatter_about(keys[0], (TABLES, SLOTS, D), 1.0, 6.0, ((0, 8), (1, 4))),
        "cotangent": scatter_about(keys[1], (TABLES, SLOTS, D), 1.0, 6.0, ((0, 8), (1, 4))),
        "w_query": scatter_about(keys[2], (D, D), D ** -0.5, 0.21875),
        "w_key": scatter_about(keys[3], (D, D), D ** -0.5, 0.21875),
        "w_value": scatter_about(keys[4], (D, D), D ** -0.5, 0.21875),
        "w_out": scatter_about(keys[5], (D, D), (D // 64) ** -0.5, 1.75),
        "w_up": scatter_about(keys[6], (D, FF), D ** -0.5, 0.21875),
        "w_down": scatter_about(keys[7], (FF, D), FF ** -0.5, 0.109375),
        "b_up": scatter_about(keys[8], (FF,), 0.5, 3.0, (), jnp.float32),
        "b_down": scatter_about(keys[9], (D,), 0.3, 2.0, (), jnp.float32),
        "g_one": jnp.clip(1.0 + 0.1 * jax.random.normal(keys[10], (D,), jnp.float32), 0.5, 1.5),
        "b_one": scatter_about(keys[11], (D,), 0.3, 2.0, (), jnp.float32),
        "g_two": jnp.clip(1.0 + 0.1 * jax.random.normal(keys[12], (D,), jnp.float32), 0.5, 1.5),
        "b_two": scatter_about(keys[13], (D,), 0.3, 2.0, (), jnp.float32),
        "ctx_count": touch_ends(jax.random.randint(keys[14], (TABLES,), SLOTS // 2, 3 * SLOTS // 4 + 1), jax.random.fold_in(keys[14], 1), SLOTS // 2, (3 * SLOTS // 4 + 1) - 1).astype(jnp.int32),
        "qry_count": touch_ends(jax.random.randint(keys[15], (TABLES,), SLOTS // 8, SLOTS // 4 + 1), jax.random.fold_in(keys[15], 1), SLOTS // 8, (SLOTS // 4 + 1) - 1).astype(jnp.int32),
        "key_keep": draw_key_keep(jax.random.fold_in(keys[17], 71), 0),
    }


@jax.custom_vjp
def low(v):
    return lax.optimization_barrier(v.astype(jnp.bfloat16)).astype(jnp.float32)

@jax.custom_vjp
def low_back(v):
    return v

def low_keep(v):
    return (low(v), None)

def low_pass(kept, grad):
    return (grad,)

def back_keep(v):
    return (v, None)

def back_low(kept, grad):
    return (low(grad),)
low.defvjp(low_keep, low_pass)
low_back.defvjp(back_keep, back_low)
precise = lax.Precision.HIGHEST
epsilon = 1e-05

def layer_norm(values, gain_vec, shift_vec):
    row_mean = lax.optimization_barrier(jnp.mean(values, axis=-1, keepdims=True))
    centred = values - row_mean
    spread = lax.optimization_barrier(jnp.mean(centred * centred, axis=-1, keepdims=True))
    return centred * lax.rsqrt(spread + epsilon) * gain_vec + shift_vec

def one_table(inputs_one, weights):
    row_data, ctx_one, qry_one, keep_one = inputs_one
    w_query, w_key, w_value, w_out, w_up, w_down, b_up, b_down, g_one, b_one, g_two, b_two = weights
    position = jnp.arange(SLOTS, dtype=jnp.int32)
    key_ok = (position < ctx_one) & (keep_one == 1)
    row_ok = position < ctx_one + qry_one
    normed = low(layer_norm(row_data, g_one, b_one))
    queries = low_back(low(jnp.dot(normed, w_query, precision=precise)))
    key_rows = low_back(low(jnp.dot(normed, w_key, precision=precise)))
    value_rows = low_back(low(jnp.dot(normed, w_value, precision=precise)))
    q_heads = queries.reshape(SLOTS, H, DH)
    k_heads = key_rows.reshape(SLOTS, H, DH)
    v_heads = value_rows.reshape(SLOTS, H, DH)
    scores = low_back(jnp.einsum('qhd,khd->hqk', q_heads, k_heads, precision=precise) * DH ** (-0.5))
    scores = jnp.where(key_ok[None, None, :], scores, -1e+30)
    highest = lax.optimization_barrier(jnp.max(scores, axis=-1, keepdims=True))
    exp_scores = jnp.exp(scores - highest)
    probs_full = exp_scores / lax.optimization_barrier(jnp.sum(exp_scores, axis=-1, keepdims=True))
    mixed_out = jnp.einsum('hqk,khd->qhd', low(probs_full), v_heads, precision=precise).reshape(SLOTS, D)
    mixed_out = low_back(low(mixed_out))
    first_sum = row_data + low_back(jnp.dot(mixed_out, w_out, precision=precise))
    normed_two = low(layer_norm(first_sum, g_two, b_two))
    hidden = low_back(jnp.dot(normed_two, w_up, precision=precise) + b_up)
    active = low(jax.nn.gelu(hidden, approximate=True))
    second_sum = first_sum + low_back(jnp.dot(active, w_down, precision=precise)) + b_down
    return jnp.where(row_ok[:, None], second_sum, 0.0)

def reference(table_rows, cotangent, w_query, w_key, w_value, w_out, w_up, w_down, b_up, b_down, g_one, b_one, g_two, b_two, ctx_count, qry_count, key_keep):
    params = tuple((param.astype(jnp.float32) for param in (w_query, w_key, w_value, w_out, w_up, w_down, b_up, b_down, g_one, b_one, g_two, b_two)))

    def forward(row_data, weights):
        table_fn = jax.checkpoint(lambda inputs_one: one_table(inputs_one, weights))
        return lax.map(table_fn, (row_data, ctx_count, qry_count, key_keep))
    result, pull = jax.vjp(forward, table_rows.astype(jnp.float32), params)
    d_input, d_params = pull(cotangent.astype(jnp.float32))
    return (result.astype(jnp.bfloat16), d_input.astype(jnp.bfloat16), d_params[0], d_params[1], d_params[2], d_params[3], d_params[4], d_params[5], d_params[6], d_params[7], d_params[8], d_params[9], d_params[10], d_params[11])
```

```python
import jax
import jax.numpy as jnp
from jax import lax
from jax.sharding import PartitionSpec as P

H = 12
DH = 64
epsilon = 1e-05
BF = jnp.bfloat16
F32 = jnp.float32


def ln_parts(values):
    row_mean = jnp.mean(values, axis=-1, keepdims=True)
    centred = values - row_mean
    spread = jnp.mean(centred * centred, axis=-1, keepdims=True)
    inv = lax.rsqrt(spread + epsilon)
    return centred * inv, inv


def ln_back(cot, xhat, inv, gain):
    a = cot * gain
    mean_a = jnp.mean(a, axis=-1, keepdims=True)
    mean_ax = jnp.mean(a * xhat, axis=-1, keepdims=True)
    return inv * (a - mean_a - xhat * mean_ax)


def gelu_tanh(values):
    return jax.nn.gelu(values, approximate=True)


def dot(a, b, ca, cb):
    return lax.dot_general(a, b, (((ca,), (cb,)), ((), ())), preferred_element_type=F32)


class Wires:
    def __init__(self, mesh):
        self.ng, self.nr = mesh.shape["grp"], mesh.shape["rows"]
        self.gbits = self.ng.bit_length() - 1
        self.rbits = self.nr.bit_length() - 1

    def flip(self, value, stage):
        axis, bit = stage
        size = self.ng if axis == "grp" else self.nr
        pairs = [(i, i ^ (1 << bit)) for i in range(size)]
        return lax.ppermute(value, axis, pairs)

    def mine(self, stage):
        axis, bit = stage
        return (lax.axis_index(axis) >> bit) & 1

    def halve(self, value, stage, axis=0):
        b = self.mine(stage)
        send = lax.dynamic_index_in_dim(value, 1 - b, axis, keepdims=False).astype(BF)
        keep = lax.dynamic_index_in_dim(value, b, axis, keepdims=False)
        got = self.flip(send, stage)
        return (keep.astype(F32) + got.astype(F32)).astype(BF)

    def double(self, value, stage, axis=0):
        got = self.flip(value, stage)
        b = self.mine(stage)
        first = jnp.where(b == 0, value, got)
        second = jnp.where(b == 0, got, value)
        return jnp.stack([first, second], axis)

    def sum_all(self, value):
        core, x = ("grp", 0), [("grp", b) for b in range(1, self.gbits)]
        y, z = ("rows", 0), [("rows", b) for b in range(1, self.rbits)]
        assert len(x) == 1
        x = x[0]
        nz = len(z)
        r, c = value.shape[-2:]
        v = value.reshape((2, 2, 2, 2) + (2,) * nz + (-1, c))
        v = self.halve(v, core, 1)
        a, b = v[0], v[1]
        a, b = self.halve(a, x), self.halve(b, y)
        a, b = self.halve(a, y), self.halve(b, x)
        v = jnp.stack([a, b])
        for s in z:
            v = self.halve(v, s, 1)
        for s in z[::-1]:
            v = self.double(v, s, 1)
        a, b = v[0], v[1]
        a, b = self.double(a, y), self.double(b, x)
        a, b = self.double(a, x), self.double(b, y)
        v = jnp.stack([a, b])
        v = self.double(v, core, 1)
        return v.reshape(value.shape)


def head_part(matrix, first_head, group_size):
    return matrix[:, first_head * DH : (first_head + group_size) * DH].reshape(
        matrix.shape[0], group_size, DH
    )


def masked_scores(q_part, k_part, key_ok):
    scores = jnp.einsum("qhd,khd->hqk", q_part, k_part, preferred_element_type=F32) * DH ** (-0.5)
    return jnp.where(key_ok[None, None, :], scores, -1e30)


def attend_forward(queries, key_rows, value_rows, key_ok, group_size):
    pieces, highest_all, totals_all = ([], [], [])
    for h in range(0, H, group_size):
        q, k, v = (head_part(m, h, group_size) for m in (queries, key_rows, value_rows))
        scores = masked_scores(q, k, key_ok)
        highest = jnp.max(scores, axis=-1, keepdims=True)
        exp_scores = jnp.exp(scores - highest)
        total = jnp.sum(exp_scores, axis=-1, keepdims=True)
        probs_low = (exp_scores / total).astype(BF)
        mixed = jnp.einsum("hqk,khd->qhd", probs_low, v, preferred_element_type=F32)
        pieces.append(mixed.reshape(queries.shape[0], group_size * DH))
        highest_all.append(highest)
        totals_all.append(total)
    return jnp.concatenate(pieces, axis=1).astype(BF), highest_all, totals_all


def attend_backward(queries, key_rows, value_rows, key_ok, d_mixed, highs, totals, group_size):
    scale = DH ** (-0.5)
    qs, ks, vs = ([], [], [])
    for i, h in enumerate(range(0, H, group_size)):
        q, k, v, g = (head_part(m, h, group_size) for m in (queries, key_rows, value_rows, d_mixed))
        scores = masked_scores(q, k, key_ok)
        probs = jnp.exp(scores - highs[i]) / totals[i]
        probs_low = probs.astype(BF)
        d_probs = jnp.einsum("qhd,khd->hqk", g, v, preferred_element_type=F32)
        inner = jnp.sum(probs * d_probs, axis=-1, keepdims=True)
        d_scores = jnp.where(key_ok[None, None, :], probs * (d_probs - inner), 0.0).astype(BF)
        dq = jnp.einsum("hqk,khd->qhd", d_scores, k, preferred_element_type=F32) * scale
        dk = jnp.einsum("hqk,qhd->khd", d_scores, q, preferred_element_type=F32) * scale
        dv = jnp.einsum("hqk,qhd->khd", probs_low, g, preferred_element_type=F32)
        qs.append(dq.reshape(queries.shape[0], group_size * DH))
        ks.append(dk.reshape(key_rows.shape[0], group_size * DH))
        vs.append(dv.reshape(key_rows.shape[0], group_size * DH))
    return tuple(jnp.concatenate(m, axis=1).astype(BF) for m in (qs, ks, vs))


def solution(mesh):
    wires = Wires(mesh)

    def shards(
        table_rows, cotangent, w_query, w_key, w_value, w_out, w_up, w_down,
        b_up, b_down, g_one, b_one, g_two, b_two, ctx_count, qry_count, key_keep,
    ):
        tables, local, width = table_rows.shape
        assert tables == 1
        ng = wires.ng
        slots = key_keep.shape[1]
        ff = w_up.shape[1]
        me = lax.axis_index("grp")
        position = me * local + jnp.arange(local, dtype=jnp.int32)
        row_mask = (position < ctx_count[0] + qry_count[0])[:, None]
        order = jnp.arange(ng, dtype=jnp.int32) ^ me
        slot_of = (order[:, None] * local + jnp.arange(local, dtype=jnp.int32)[None, :]).reshape(-1)
        keep = jnp.take(key_keep[0].reshape(ng, local), order, axis=0).reshape(-1)
        key_ok = (slot_of < ctx_count[0]) & (keep == 1)

        rows_bf = table_rows[0]
        across = wires.flip(rows_bf, ("grp", 1))
        beside = wires.flip(rows_bf, ("grp", 0))
        corner = wires.flip(across, ("grp", 0))
        all_rows = jnp.concatenate([rows_bf, beside, across, corner], axis=0).astype(F32)
        row_data = rows_bf.astype(F32)
        xhat_all, inv_all = ln_parts(all_rows)
        normed_all = (xhat_all * g_one + b_one).astype(BF)
        normed = normed_all[:local]
        queries = dot(normed, w_query, 1, 0).astype(BF)
        key_rows = dot(normed_all, w_key, 1, 0).astype(BF)
        value_rows = dot(normed_all, w_value, 1, 0).astype(BF)

        mixed, highs, totals = attend_forward(queries, key_rows, value_rows, key_ok, 4)
        first_sum = row_data + dot(mixed, w_out, 1, 0)
        xhat2, inv2 = ln_parts(first_sum)
        normed_two = (xhat2 * g_two + b_two).astype(BF)
        hidden = dot(normed_two, w_up, 1, 0) + b_up
        active = gelu_tanh(hidden).astype(BF)
        second_sum = first_sum + dot(active, w_down, 1, 0) + b_down
        result = jnp.where(row_mask, second_sum, 0.0).astype(BF)

        grad_low = jnp.where(row_mask, cotangent[0], jnp.zeros((), BF))
        grad_out = grad_low.astype(F32)
        d_w_down = dot(active, grad_low, 0, 0)
        sum_down = wires.sum_all(d_w_down.astype(BF).reshape(64, ff // 64, width))
        d_b_down = jnp.sum(grad_out, axis=0)
        d_active = dot(grad_low, w_down, 1, 1)
        d_hidden = jax.vjp(gelu_tanh, hidden)[1](d_active)[0].astype(BF)
        d_b_up = jnp.sum(d_hidden, axis=0, dtype=F32)
        d_w_up = dot(normed_two, d_hidden, 0, 0)
        up_blocks = d_w_up.astype(BF).reshape(2, 4, width // 8, 8, ff // 8)
        up_blocks = up_blocks.transpose(0, 3, 1, 2, 4)
        sum_up = wires.sum_all(up_blocks.reshape(64, width // 8, ff // 8))
        d_normed_two = dot(d_hidden, w_up, 1, 1)
        d_g_two = jnp.sum(d_normed_two * xhat2, axis=0)
        d_b_two = jnp.sum(d_normed_two, axis=0)
        d_first = grad_out + ln_back(d_normed_two, xhat2, inv2, g_two)
        d_first_low = d_first.astype(BF)
        d_w_out = dot(mixed, d_first_low, 0, 0)
        d_mixed = dot(d_first_low, w_out, 1, 1).astype(BF)

        d_query, d_keys, d_values = attend_backward(
            queries, key_rows, value_rows, key_ok, d_mixed, highs, totals, 4
        )
        d_w_query = dot(normed, d_query, 0, 0)
        d_w_key = dot(normed_all, d_keys, 0, 0)
        d_w_value = dot(normed_all, d_values, 0, 0)
        cot = dot(d_keys, w_key, 1, 1) + dot(d_values, w_value, 1, 1)
        cot = jnp.concatenate([cot[:local] + dot(d_query, w_query, 1, 1), cot[local:]], axis=0)
        d_g_one = jnp.sum(cot * xhat_all, axis=0)
        d_b_one = jnp.sum(cot, axis=0)

        c4 = cot.reshape(2, 2, local, width)
        got = wires.flip(c4[:, 1].astype(BF), ("grp", 0))
        pair = c4[:, 0] + got.astype(F32)
        got = wires.flip(pair[1].astype(BF), ("grp", 1))
        d_normed = pair[0] + got.astype(F32)
        d_rows = (d_first + ln_back(d_normed, xhat_all[:local], inv_all[:local], g_one)).astype(BF)

        vec = jnp.concatenate([d_b_up, d_b_down, d_g_one, d_b_one, d_g_two, d_b_two])
        n_vec = vec.shape[0]
        vec = jnp.pad(vec, (0, 64 * 8 * width - n_vec)).astype(BF).reshape(64, 8, width)
        square = jnp.concatenate([d_w_query, d_w_key, d_w_value, d_w_out], axis=0).astype(BF)
        square = square.reshape(64, -1, width)
        tail = wires.sum_all(jnp.concatenate([square, vec], axis=1))
        per = square.shape[1]
        sums = tail[:, :per].reshape(4, width, width).astype(F32)
        flat = tail[:, per:].reshape(-1)[:n_vec].astype(F32)
        f_up, f_rest = flat[:ff], flat[ff:].reshape(5, width)
        out_up = sum_up.reshape(2, 8, 4, width // 8, ff // 8).transpose(0, 2, 3, 1, 4)
        return (
            result[None], d_rows[None],
            sums[0], sums[1], sums[2], sums[3],
            out_up.reshape(width, ff).astype(F32),
            sum_down.reshape(ff, width).astype(F32),
            f_up, f_rest[0], f_rest[1], f_rest[2], f_rest[3], f_rest[4],
        )

    rows3 = P("rows", "grp", None)
    placed = (rows3, rows3) + (P(),) * 12 + (P("rows"), P("rows"), P("rows", None))
    return jax.shard_map(
        shards, mesh=mesh, in_specs=placed, out_specs=(rows3, rows3) + (P(),) * 12, check_vma=False
    )
```

```python
import functools

import jax
import jax.numpy as jnp
from jax import lax
from jax.experimental import pallas as pl
from jax.experimental.pallas import tpu as pltpu
from jax.sharding import PartitionSpec as P

H = 12
DH = 64
SCALE = DH**-0.5
MAX_CTX = 1536
epsilon = 1e-05
BF = jnp.bfloat16
F32 = jnp.float32


def dot(a, b, ca, cb):
    return lax.dot_general(a, b, (((ca,), (cb,)), ((), ())), preferred_element_type=F32)


def after(value, *deps):
    return lax.optimization_barrier((value,) + deps)[0]


def ln_parts(values):
    row_mean = jnp.mean(values, axis=-1, keepdims=True)
    centred = values - row_mean
    spread = jnp.mean(centred * centred, axis=-1, keepdims=True)
    inv = lax.rsqrt(spread + epsilon)
    return centred * inv, inv


def ln_back(cot, xhat, inv, gain):
    a = cot * gain
    mean_a = jnp.mean(a, axis=-1, keepdims=True)
    mean_ax = jnp.mean(a * xhat, axis=-1, keepdims=True)
    return inv * (a - mean_a - xhat * mean_ax)


def gelu_tanh(values):
    return jax.nn.gelu(values, approximate=True)


def attend_kernel(q_ref, k_ref, v_ref, bias_ref, o_ref, m_ref, l_ref, *, tq):
    lane = lax.broadcasted_iota(jnp.int32, (1, 128), 1)
    for i in range(q_ref.shape[0] // tq):
        rows = slice(i * tq, (i + 1) * tq)
        q = q_ref[rows, :] * jnp.asarray(SCALE, BF)
        scored, outs = [], []
        for h in range(2):
            qm = jnp.where(lane // DH == h, q, jnp.zeros((), BF))
            s = dot(qm, k_ref[...], 1, 1) + bias_ref[...]
            scored.append((s, jnp.max(s, axis=1, keepdims=True)))
        for h in range(2):
            s, m = scored[h]
            p = jnp.exp(s - m)
            total = jnp.sum(p, axis=1, keepdims=True)
            outs.append(dot(p.astype(BF), v_ref[...], 1, 0) / total)
            m_ref[0, h : h + 1, rows] = jnp.broadcast_to(m, (tq, 128)).T[0:1]
            l_ref[0, h : h + 1, rows] = jnp.broadcast_to(total, (tq, 128)).T[0:1]
        o_ref[rows, :] = jnp.where(lane < DH, outs[0], outs[1]).astype(BF)


def attend(q, k, v, bias):
    nq, width = q.shape
    nk, pairs = k.shape[0], width // 128
    col = lambda n: pl.BlockSpec((n, 128), lambda j: (0, j))
    stat = pl.BlockSpec((1, 2, nq), lambda j: (j, 0, 0))
    return pl.pallas_call(
        functools.partial(attend_kernel, tq=256),
        grid=(pairs,),
        in_specs=[col(nq), col(nk), col(nk), pl.BlockSpec((1, nk), lambda j: (0, 0))],
        out_specs=[col(nq), stat, stat],
        out_shape=[
            jax.ShapeDtypeStruct((nq, width), BF),
            jax.ShapeDtypeStruct((pairs, 2, nq), F32),
            jax.ShapeDtypeStruct((pairs, 2, nq), F32),
        ],
        compiler_params=pltpu.CompilerParams(vmem_limit_bytes=56 << 20),
        cost_estimate=pl.CostEstimate(
            flops=16 * nq * nk * width, bytes_accessed=8 * nk * width, transcendentals=nq * nk * width // DH
        ),
        name="attend",
    )(q, k, v, bias)


def attend_back_kernel(
    q_ref, k_ref, v_ref, bias_ref, do_ref, o_ref, m_ref, l_ref, dq_ref, dk_ref, dv_ref, ds_scr, *, tk
):
    nq, nk = q_ref.shape[0], k_ref.shape[0]
    lane = lax.broadcasted_iota(jnp.int32, (1, 128), 1)
    k_t = k_ref[...].T
    dof = do_ref[...].astype(F32)
    prod_t = (dof * o_ref[...].astype(F32)).T
    qs = q_ref[...] * jnp.asarray(SCALE, BF)
    dks, dvs, dqs = [], [], []
    for h in range(2):
        own = lane // DH == h
        qm = jnp.where(own, qs, jnp.zeros((), BF))
        m = m_ref[0, h : h + 1, :]
        inv = 1.0 / l_ref[0, h : h + 1, :]
        delta = jnp.sum(prod_t[h * DH : (h + 1) * DH], axis=0, keepdims=True) * inv
        dom = jnp.where(own, dof * jnp.broadcast_to(inv, (128, nq)).T, 0.0).astype(BF)
        for c in range(nk // tk):
            sl = slice(c * tk, (c + 1) * tk)
            s = dot(k_ref[sl, :], qm, 1, 1)
            p = jnp.exp(s + jnp.concatenate([bias_ref[sl, :]] * (nq // 128), axis=1) - m)
            dp = dot(v_ref[sl, :], dom, 1, 1)
            ds = (p * (dp - delta)).astype(BF)
            ds_scr[h, sl, :] = ds
            dv = dot(p.astype(BF), dom, 1, 0)
            dk = dot(ds, qm, 1, 0)
            if h == 0:
                dks.append(dk)
                dvs.append(dv)
            else:
                dk_ref[sl, :] = (dks[c] + dk).astype(BF)
                dv_ref[sl, :] = (dvs[c] + dv).astype(BF)
        dqs.append(dot(k_t[h * DH : (h + 1) * DH, :], ds_scr[h], 1, 0) * SCALE)
    dq_ref[...] = jnp.concatenate(dqs, axis=0).T.astype(BF)


def attend_back(q, k, v, bias, do, o, m, total, first, pairs):
    nq, nk = q.shape[0], k.shape[0]
    col = lambda n: pl.BlockSpec((n, 128), lambda j: (0, j + first))
    out = lambda n: pl.BlockSpec((n, 128), lambda j: (0, j))
    stat = pl.BlockSpec((1, 2, nq), lambda j: (j + first, 0, 0))
    wide = pairs * 128
    return pl.pallas_call(
        functools.partial(attend_back_kernel, tk=256),
        grid=(pairs,),
        in_specs=[
            col(nq), col(nk), col(nk), pl.BlockSpec((nk, 128), lambda j: (0, 0)), col(nq), col(nq), stat, stat,
        ],
        out_specs=[out(nq), out(nk), out(nk)],
        out_shape=[
            jax.ShapeDtypeStruct((nq, wide), BF),
            jax.ShapeDtypeStruct((nk, wide), BF),
            jax.ShapeDtypeStruct((nk, wide), BF),
        ],
        scratch_shapes=[pltpu.VMEM((2, nk, nq), BF)],
        compiler_params=pltpu.CompilerParams(vmem_limit_bytes=56 << 20),
        cost_estimate=pl.CostEstimate(
            flops=40 * nq * nk * wide, bytes_accessed=12 * nk * wide, transcendentals=nq * nk * wide // DH
        ),
        name="attend_back",
    )(q, k, v, bias, do, o, m, total)


class Wires:
    def __init__(self, mesh):
        self.ng, self.nr = mesh.shape["grp"], mesh.shape["rows"]
        assert self.ng == 4
        rbits = self.nr.bit_length() - 1
        self.core, self.x, self.y = ("grp", 0), ("grp", 1), ("rows", 0)
        self.z = [("rows", b) for b in range(1, rbits)]

    def flip(self, value, stage):
        axis, bit = stage
        size = self.ng if axis == "grp" else self.nr
        return lax.ppermute(value, axis, [(i, i ^ (1 << bit)) for i in range(size)])

    def mine(self, stage):
        axis, bit = stage
        return (lax.axis_index(axis) >> bit) & 1

    def halve(self, value, stage, axis=0):
        b = self.mine(stage)
        half = value.shape[axis] // 2
        send = lax.dynamic_slice_in_dim(value, (1 - b) * half, half, axis).astype(BF)
        keep = lax.dynamic_slice_in_dim(value, b * half, half, axis)
        got = self.flip(send, stage)
        return (keep.astype(F32) + got.astype(F32)).astype(BF)

    def double(self, value, stage, axis=0):
        got = self.flip(value, stage)
        b = self.mine(stage)
        return jnp.concatenate([jnp.where(b == 0, value, got), jnp.where(b == 0, got, value)], axis)

    def scatter(self, value):
        r, c = value.shape
        v = value.reshape(2, 8, r // 16, c)
        v = self.halve(v, self.core, 1)
        a, b = self.halve(v[0], self.x), self.halve(v[1], self.y)
        a, b = self.halve(a, self.y), self.halve(b, self.x)
        v = jnp.concatenate([a, b])
        for i, s in enumerate(self.z):
            v = self.halve(v, s, 2 - i % 2)
        return v

    def gather(self, v, r):
        for i, s in list(enumerate(self.z))[::-1]:
            v = self.double(v, s, 2 - i % 2)
        a, b = self.double(v[:1], self.y), self.double(v[1:], self.x)
        a, b = self.double(a, self.x), self.double(b, self.y)
        v = self.double(jnp.stack([a, b]), self.core, 1)
        return v.reshape(r, -1)


def solution(mesh):
    wires = Wires(mesh)

    def shards(
        table_rows, cotangent, w_query, w_key, w_value, w_out, w_up, w_down,
        b_up, b_down, g_one, b_one, g_two, b_two, ctx_count, qry_count, key_keep,
    ):
        tables, local, width = table_rows.shape
        assert tables == 1
        ng = wires.ng
        slots = key_keep.shape[1]
        ff = w_up.shape[1]
        groups = min(ng, -(-MAX_CTX // local))
        keys = groups * local
        me = lax.axis_index("grp")
        ctx, qry = ctx_count[0], qry_count[0]
        position = me * local + jnp.arange(local, dtype=jnp.int32)
        row_mask = (position < ctx + qry)[:, None]
        key_ok = (jnp.arange(keys, dtype=jnp.int32) < ctx) & (key_keep[0, :keys] == 1)
        bias = jnp.where(key_ok, 0.0, -1e30).astype(F32)
        no_key = jnp.logical_not(jnp.any(key_ok))
        bias_row = bias[None, :]
        bias_col = jnp.broadcast_to(bias[:, None], (keys, 128))

        rows_bf = table_rows[0]
        across = wires.flip(rows_bf, wires.x)
        beside = wires.flip(rows_bf, wires.core)
        corner = wires.flip(across, wires.core)
        near = jnp.stack([rows_bf, beside, across, corner])
        pick = lambda i: lax.dynamic_index_in_dim(near, i ^ me, 0, keepdims=False)
        norm = lambda rows: (ln_parts(rows.astype(F32))[0] * g_one + b_one).astype(BF)
        row_data = rows_bf.astype(F32)
        xhat, inv = ln_parts(row_data)
        normed = (xhat * g_one + b_one).astype(BF)
        queries = dot(normed, w_query, 1, 0).astype(BF)
        normed_keys = norm(jnp.concatenate([pick(i) for i in range(groups)]))
        key_rows = dot(normed_keys, w_key, 1, 0).astype(BF)
        value_rows = dot(normed_keys, w_value, 1, 0).astype(BF)

        mixed, high, total = attend(queries, key_rows, value_rows, bias_row)

        def uniform():
            everything = norm(near.reshape(-1, width))
            values = dot(everything, w_value, 1, 0).astype(BF).astype(F32)
            mean = jnp.mean(values, axis=0, keepdims=True).astype(BF)
            return jnp.broadcast_to(mean, mixed.shape)

        mixed = lax.cond(no_key, uniform, lambda: mixed)
        first_sum = row_data + dot(mixed, w_out, 1, 0)
        xhat2, inv2 = ln_parts(first_sum)
        normed_two = (xhat2 * g_two + b_two).astype(BF)
        hidden = dot(normed_two, w_up, 1, 0) + b_up
        active = gelu_tanh(hidden).astype(BF)
        grad_low = jnp.where(row_mask, cotangent[0], jnp.zeros((), BF))
        grad_out = grad_low.astype(F32)
        d_w_down = dot(active, grad_low, 0, 0).astype(BF)
        part_down = wires.scatter(d_w_down)

        grad_low2 = after(grad_low, d_w_down)
        d_active = dot(grad_low2, w_down, 1, 1)
        d_hidden = jax.vjp(gelu_tanh, hidden)[1](d_active)[0].astype(BF)
        d_normed_two = dot(d_hidden, w_up, 1, 1)
        d_first = grad_out + ln_back(d_normed_two, xhat2, inv2, g_two)
        d_first_low = d_first.astype(BF)
        d_w_up = dot(normed_two, d_hidden, 0, 0).astype(BF)
        d_w_out = dot(mixed, d_first_low, 0, 0).astype(BF)
        d_up_out = jnp.concatenate([d_w_up, d_w_out], axis=1)
        part_up = wires.scatter(d_up_out)

        d_mixed = dot(d_first_low, w_out, 1, 1).astype(BF)
        d_mixed = after(d_mixed, d_up_out)
        second_sum = first_sum + dot(active, w_down, 1, 0) + b_down
        result = jnp.where(row_mask, second_sum, 0.0).astype(BF)

        pairs = width // 128
        sizes = [pairs - pairs // 2, pairs // 2]
        parts, first = [], 0
        for n in sizes:
            parts.append(
                attend_back(queries, key_rows, value_rows, bias_col, d_mixed, mixed, high, total, first, n)
            )
            first += n
        dq, dk, dv = (jnp.concatenate([p[i] for p in parts], axis=1) for i in range(3))

        def uniform_back():
            flat = jnp.sum(d_mixed.astype(F32), axis=0, keepdims=True) / slots
            flat = flat.astype(BF)
            return jnp.zeros_like(dq), jnp.zeros_like(dk), jnp.broadcast_to(flat, dv.shape), flat

        dq, dk, dv, flat = lax.cond(
            no_key, uniform_back, lambda: (dq, dk, dv, jnp.zeros((1, width), BF))
        )
        d_w_query = dot(normed, dq, 0, 0)
        d_w_key = dot(normed_keys, dk, 0, 0)
        d_w_value = dot(normed_keys, dv, 0, 0)
        sum_q, sum_k, sum_v = (jnp.sum(m.astype(F32), axis=0) for m in (dq, dk, dv))
        n_rest = ng - groups
        rest = []
        if n_rest:
            def rest_terms():
                far = norm(jnp.concatenate([pick(i) for i in range(groups, ng)]))
                wide = jnp.broadcast_to(flat, far.shape)
                return dot(far, wide, 0, 0)

            d_w_value = d_w_value + lax.cond(no_key, rest_terms, lambda: jnp.zeros((width, width), F32))
            sum_v = sum_v + flat[0].astype(F32) * (n_rest * local)
            rest = [jnp.broadcast_to(dot(flat, w_value, 1, 1), (local, width))] * n_rest
        lean = lambda w, s: jnp.sum(w.astype(F32) * s[None, :], axis=1)
        d_b_one = lean(w_query, sum_q) + lean(w_key, sum_k) + lean(w_value, sum_v)
        joint = lambda w, g: jnp.sum(w.astype(F32) * g, axis=1)
        d_g_one = joint(w_query, d_w_query) + joint(w_key, d_w_key) + joint(w_value, d_w_value)
        d_g_one = (d_g_one - b_one * d_b_one) / g_one

        d_b_up = jnp.sum(d_hidden, axis=0, dtype=F32)
        d_b_down = jnp.sum(grad_out, axis=0)
        d_g_two = jnp.sum(d_normed_two * xhat2, axis=0)
        d_b_two = jnp.sum(d_normed_two, axis=0)
        vec = jnp.concatenate([d_b_up, d_b_down, d_g_one, d_b_one, d_g_two, d_b_two])
        n_vec = vec.shape[0]
        n_row = -(-n_vec // (16 * 256))
        vec = jnp.pad(vec, (0, 16 * 256 * n_row - n_vec)).reshape(16, n_row, 256)
        vec = jnp.pad(vec, ((0, 0), (0, width // 16 - n_row), (0, 0))).reshape(width, 256)
        tail = jnp.concatenate([m.astype(BF) for m in (d_w_query, d_w_key, d_w_value, vec)], axis=1)
        part_tail = wires.scatter(tail)

        dk2, dv2 = (after(m, tail) for m in (dk, dv))
        cot = dot(dk2, w_key, 1, 1) + dot(dv2, w_value, 1, 1)
        c4 = jnp.concatenate([cot] + rest).reshape(ng, local, width)
        block = lambda j: lax.dynamic_index_in_dim(c4, me ^ j, 0, keepdims=False)
        got = wires.flip(jnp.stack([block(1), block(3)]).astype(BF), wires.core)
        far = (block(2) + got[1].astype(F32)).astype(BF)
        got2 = wires.flip(far, wires.x)
        d_normed = dot(dq, w_query, 1, 1) + block(0) + got[0].astype(F32) + got2.astype(F32)
        d_rows = (d_first + ln_back(d_normed, xhat, inv, g_one)).astype(BF)

        sum_down = wires.gather(part_down, ff)
        sum_up = wires.gather(part_up, width)
        sum_tail = wires.gather(part_tail, width)
        up, out = sum_up[:, :ff], sum_up[:, ff:]
        flat_sum = sum_tail[:, 3 * width :].reshape(16, -1, 256)[:, :n_row].reshape(-1)[:n_vec].astype(F32)
        f_up, f_rest = flat_sum[:ff], flat_sum[ff:].reshape(5, width)
        square = [sum_tail[:, i * width : (i + 1) * width].astype(F32) for i in range(3)]
        return (
            result[None], d_rows[None],
            square[0], square[1], square[2], out.astype(F32),
            up.astype(F32), sum_down.astype(F32),
            f_up, f_rest[0], f_rest[1], f_rest[2], f_rest[3], f_rest[4],
        )

    rows3 = P("rows", "grp", None)
    placed = (rows3, rows3) + (P(),) * 12 + (P("rows"), P("rows"), P("rows", None))
    return jax.shard_map(
        shards, mesh=mesh, in_specs=placed, out_specs=(rows3, rows3) + (P(),) * 12, check_vma=False
    )
```
